256 devices in a mesh: row: 32 (over z_lo, y, core), col: 8 (over x, z_hi).
Axes of the slice: x: 4, y: 4, z: 8 (z_hi: 2, z_lo: 4; z = z_hi * 4 + z_lo), core: 2. Of those that a mesh axis runs over, the one named last changes fastest.
Arguments:
- object_field: float32 [2, 8192, 2048], P(None, 'row', 'col'), may hold values from -6 to 6
- probe_field: float32 [2, 256, 256], replicated, may hold values from -6 to 6
- intensity: float32 [32, 8, 4, 256, 256], P('row', 'col'), may hold values from 0.25 to 16
- view_offsets: int32 [32, 8, 4, 2], P('row', 'col'), may hold values from 0 to 128
- view_counts: int32 [32, 8], P('row', 'col'), may hold values from 1 to 4, as said below
Outputs:
- updated_object: float32 [2, 8192, 2048], P(None, 'row', 'col')
The draws below stay inside these ranges and needn't reach their ends.
Inputs may be any that keep to these rules, and one draw needn't show every extreme that they name: `view_counts`: every draw has some tile with 4 valid views. `view_offsets`: each view lies inside its tile's padded window.
All inputs are finite; a program needn't handle non-finite values.
Results may differ from the reference program's by a relative error of at most 0.0003.
Values sent between devices are 32-bit elements; how exact they have to be, the bound alone decides.
A program may use at most 64 MiB of HBM per device.

```python
import math
import jax
import jax.numpy as jnp
from jax import lax

CORE = 256
MARGIN = 64
PROBE = 256
VIEWS = 4
NR = 8192
NC = 2048
N_ROW = 32
N_COL = 8


def draw_view_counts(key, part):
    drawn_counts = jax.random.randint(key, (N_ROW * N_COL,), 1, VIEWS + 1)
    chosen_tile = jax.random.randint(jax.random.fold_in(key, 7), (), 0, N_ROW * N_COL)
    flattened = jnp.where(jnp.arange(N_ROW * N_COL) == chosen_tile, VIEWS, drawn_counts)
    return flattened.reshape(N_ROW, N_COL).astype(jnp.int32)


def plant(drawn, rng, least, largest):
    longest = drawn.shape.index(max(drawn.shape))
    spots = []
    for shift in (0, 1):
        where = [jax.random.randint(jax.random.fold_in(rng, axis), (), 0, length) for axis, length in enumerate(drawn.shape)]
        where[longest] = (where[longest] + shift) % drawn.shape[longest]
        spots.append(tuple(where))
    return drawn.at[spots[0]].set(least).at[spots[1]].set(largest)


def steps_of(stream_key, extent, pieces, low, top_value):
    gain = 1.0
    for axis_at, parts in pieces:
        draws = jax.random.uniform(jax.random.fold_in(jax.random.fold_in(stream_key, 6), axis_at), (parts,), jnp.float32, low / len(pieces), top_value / len(pieces))
        gain = gain * jnp.repeat(jnp.exp(draws), extent[axis_at] // parts).reshape((-1,) + (1,) * (len(extent) - 1 - axis_at))
    return gain


def gaussian(stream_key, shape, width, reach, pieces=(), held_as=jnp.bfloat16):
    factor_of = steps_of(stream_key, shape, pieces, -0.22, 0.18) if pieces else 1.0
    result = jax.random.normal(stream_key, shape, jnp.float32) * width * factor_of
    return jnp.minimum(jnp.maximum(result, -reach), reach).astype(held_as)


def setup_inputs(seed: int = 0) -> dict:
    arg_keys = jax.random.split(jax.random.key(seed), 6)
    return {
        "object_field": gaussian(arg_keys[0], (2, NR, NC), 1.0, 6.0, ((1, 32), (2, 8)), jnp.float32),
        "probe_field": gaussian(arg_keys[1], (2, PROBE, PROBE), 1.0, 6.0, (), jnp.float32),
        "intensity": jnp.clip(jnp.exp(math.log(16.0) - 4.158883 * jax.random.uniform(arg_keys[2], (N_ROW, N_COL, VIEWS, PROBE, PROBE), jnp.float32) ** steps_of(arg_keys[2], (N_ROW, N_COL, VIEWS, PROBE, PROBE), ((0, 32), (1, 8)), -0.2, 0.2)), 0.25, 16.0),
        "view_offsets": plant(jax.random.randint(arg_keys[3], (N_ROW, N_COL, VIEWS, 2), 0, CORE + 2 * MARGIN - PROBE + 1), jax.random.fold_in(arg_keys[3], 1), 0, CORE + 2 * MARGIN - PROBE).astype(jnp.int32),
        "view_counts": draw_view_counts(jax.random.fold_in(arg_keys[5], 71), 0),
    }


smooth_eps = 0.1
step_size = 0.2

def tile_gradient(window, probe_field, measured, offsets, active):
    probe_len = probe_field.shape[-1]
    wave_probe = lax.complex(probe_field[0], probe_field[1])
    gradient = jnp.zeros_like(window)
    for number in range(VIEWS):
        anchor = (jnp.int32(0), offsets[number, 0], offsets[number, 1])
        patch_field = lax.dynamic_slice(window, anchor, (2, probe_len, probe_len))
        exit_wave = wave_probe * lax.complex(patch_field[0], patch_field[1])
        farfield = jnp.fft.fft2(exit_wave, norm='ortho')
        modulus = jnp.sqrt(farfield.real * farfield.real + farfield.imag * farfield.imag + smooth_eps)
        scaling = 1.0 - jnp.sqrt(measured[number] + smooth_eps) / modulus
        backward = jnp.fft.ifft2(farfield * scaling, norm='ortho')
        contrib = jnp.conj(wave_probe) * backward
        stacked = jnp.stack([contrib.real, contrib.imag])
        stacked = jnp.where(number < active, stacked, jnp.zeros_like(stacked))
        current = lax.dynamic_slice(gradient, anchor, (2, probe_len, probe_len))
        gradient = lax.dynamic_update_slice(gradient, current + stacked, anchor)
    return gradient

def reference(object_field, probe_field, intensity, view_offsets, view_counts):
    core_len = CORE
    margin_len = MARGIN
    side_len = core_len + 2 * margin_len
    padded_image = jnp.pad(object_field, ((0, 0), (margin_len, margin_len), (margin_len, margin_len)))

    def one_tile(flat_index):
        tile_row = flat_index // N_COL
        tile_col = flat_index % N_COL
        window = lax.dynamic_slice(padded_image, (jnp.int32(0), tile_row * core_len, tile_col * core_len), (2, side_len, side_len))
        return tile_gradient(window, probe_field, intensity[tile_row, tile_col], view_offsets[tile_row, tile_col], view_counts[tile_row, tile_col])
    tile_grads = lax.map(one_tile, jnp.arange(N_ROW * N_COL, dtype=jnp.int32))
    tile_grads = tile_grads.reshape(N_ROW, N_COL, 2, side_len, side_len)
    zero_pad = (0, 0)
    from_above = jnp.pad(tile_grads[:-1, :, :, core_len + margin_len:, :], ((1, 0), zero_pad, zero_pad, zero_pad, zero_pad))
    from_below = jnp.pad(tile_grads[1:, :, :, :margin_len, :], ((0, 1), zero_pad, zero_pad, zero_pad, zero_pad))
    banded = tile_grads[:, :, :, margin_len:margin_len + core_len, :]
    banded = banded.at[:, :, :, :margin_len, :].add(from_above)
    banded = banded.at[:, :, :, core_len - margin_len:, :].add(from_below)
    from_left = jnp.pad(banded[:, :-1, :, :, core_len + margin_len:], (zero_pad, (1, 0), zero_pad, zero_pad, zero_pad))
    from_right = jnp.pad(banded[:, 1:, :, :, :margin_len], (zero_pad, (0, 1), zero_pad, zero_pad, zero_pad))
    folded = banded[:, :, :, :, margin_len:margin_len + core_len]
    folded = folded.at[:, :, :, :, :margin_len].add(from_left)
    folded = folded.at[:, :, :, :, core_len - margin_len:].add(from_right)
    assembled = jnp.transpose(folded, (2, 0, 3, 1, 4)).reshape(2, N_ROW * core_len, N_COL * core_len)
    return object_field - step_size * assembled
```

```python
import functools

import jax
import jax.numpy as jnp
import ml_dtypes
import numpy as np
from jax import lax
from jax.experimental import pallas as pl
from jax.experimental.pallas import tpu as pltpu
from jax.sharding import PartitionSpec as P

MESH = pl.DeviceIdType.MESH
CORE = 256
MARGIN = 64
HALF = 128
smooth_eps = 0.1
step_size = 0.2
f32, bf16 = jnp.float32, jnp.bfloat16


def dft_tables():
    index = np.arange(HALF)
    forms = []
    for parity in (0, 1):
        turns = (index[:, None] * (2 * index[None, :] + parity)) % CORE
        entries = np.exp(-2j * np.pi * turns / CORE) / np.sqrt(CORE)
        forms.append(np.block([[entries.real, entries.imag], [-entries.imag, entries.real]]))
    forms = np.stack(forms).astype(np.float32)
    forms = np.stack([forms, np.swapaxes(forms, 1, 2)])
    high = forms.astype(ml_dtypes.bfloat16)
    low = (forms - high.astype(np.float32)).astype(ml_dtypes.bfloat16)
    return np.stack([high, low], axis=2)


def order_tables():
    move = np.zeros((CORE, CORE), np.float32)
    index = np.arange(HALF)
    move[2 * index, index] = 1.0
    move[2 * index + 1, HALF + index] = 1.0
    return np.stack([move, move.T]).astype(ml_dtypes.bfloat16)


def dot(left, right):
    return jnp.dot(left, right, preferred_element_type=f32)


def split(value):
    high = value.astype(bf16)
    return high, (value - high.astype(f32)).astype(bf16)


def times_table(value, tab, form, parity):
    high, low = split(value)
    t_high, t_low = tab[form, parity, 0], tab[form, parity, 1]
    return dot(high, t_high) + dot(low, t_high) + dot(high, t_low)


def table_times(value, tab, form, parity):
    high, low = split(value)
    t_high, t_low = tab[form, parity, 0], tab[form, parity, 1]
    return dot(t_high, high) + dot(t_high, low) + dot(t_low, high)


def lanes(*parts):
    return jnp.concatenate(parts, axis=1)


def rows(*parts):
    return jnp.concatenate(parts, axis=0)


def columns(tile):
    return slice(HALF * tile, HALF * tile + HALF)


def prepare_intensity(measured, order, scaled, number):
    right, left = order[0], order[1]
    value = measured[number]
    first = value.astype(bf16)
    rest = value - first.astype(f32)
    second = rest.astype(bf16)
    third = (rest - second.astype(f32)).astype(bf16)
    moved = [dot(left, dot(part, right).astype(bf16)) for part in (first, second, third)]
    total = (moved[0] + moved[1] + moved[2]) + smooth_eps
    scaled[number, 0] = total[:HALF]
    scaled[number, 1] = total[HALF:]


def prepare_probe(probe, rolled, number, row_off, col_off):
    for part in range(2):
        turned = pltpu.roll(probe[part], lax.rem(row_off + CORE, CORE), 0)
        rolled[number, part] = pltpu.roll(turned, lax.rem(col_off + CORE, CORE), 1)


def one_view(number, row_off, col_off, valid, core, side, ends, corner, rolled, scaled, tab, sums):
    lane = lax.broadcasted_iota(jnp.int32, (1, HALF), 1)
    line = lax.broadcasted_iota(jnp.int32, (MARGIN, 1), 0)
    in_side = (lane < col_off, lane >= HALF + col_off)
    in_low, in_high = line < row_off, line >= MARGIN + row_off

    def patch(part, tile):
        middle = jnp.where(in_side[tile], side[part], core[part, :, columns(tile)])
        outer = jnp.where(in_side[tile], corner[part], ends[part, :, columns(tile)])
        low = jnp.where(in_low, outer[:64], middle[:64])
        high = jnp.where(in_high, outer[64:], middle[192:])
        return rows(low, middle[64:192], high)

    waves = []
    for tile in range(2):
        p_re, p_im = rolled[number, 0, :, columns(tile)], rolled[number, 1, :, columns(tile)]
        o_re, o_im = patch(0, tile), patch(1, tile)
        waves.append(lanes(p_re * o_re - p_im * o_im, p_re * o_im + p_im * o_re))
    even = times_table(waves[0] + waves[1], tab, 0, 0)
    odd = times_table(waves[0] - waves[1], tab, 0, 1)

    def stacked(even_cols, odd_cols):
        return rows(
            lanes(even_cols[:, :HALF], odd_cols[:, :HALF]),
            lanes(even_cols[:, HALF:], odd_cols[:, HALF:]),
        )

    halves = (
        stacked(even[:HALF] + even[HALF:], odd[:HALF] + odd[HALF:]),
        stacked(even[:HALF] - even[HALF:], odd[:HALF] - odd[HALF:]),
    )
    back = []
    for parity in range(2):
        far = table_times(halves[parity], tab, 1, parity)
        far_re, far_im = far[:HALF], far[HALF:]
        wanted = scaled[number, parity]
        found = far_re * far_re + far_im * far_im + smooth_eps
        scaling = 1.0 - wanted * lax.rsqrt(wanted * found)
        corrected = rows(far_re * scaling, far_im * scaling)
        back.append(table_times(corrected, tab, 0, parity))
    upper, lower = back[0] + back[1], back[0] - back[1]
    re = rows(upper[:HALF], lower[:HALF])
    im = rows(upper[HALF:], lower[HALF:])
    even = times_table(lanes(re[:, :HALF], im[:, :HALF]), tab, 1, 0)
    odd = times_table(lanes(re[:, HALF:], im[:, HALF:]), tab, 1, 1)
    core_sum, side_sum, ends_sum, corner_sum = sums
    for tile, wave in ((0, even + odd), (1, even - odd)):
        b_re, b_im = wave[:, :HALF], wave[:, HALF:]
        p_re, p_im = rolled[number, 0, :, columns(tile)], rolled[number, 1, :, columns(tile)]
        for part, raw in ((0, p_re * b_re + p_im * b_im), (1, p_re * b_im - p_im * b_re)):
            grad = raw * valid
            outside = jnp.where(in_side[tile], grad, 0.0)
            inside = jnp.where(in_side[tile], 0.0, grad)
            for value, main, edge, where in (
                (inside, core_sum, ends_sum, columns(tile)),
                (outside, side_sum, corner_sum, slice(0, HALF)),
            ):
                low = jnp.where(in_low, value[:64], 0.0)
                high = jnp.where(in_high, value[192:], 0.0)
                kept = rows(value[:64] - low, value[64:192], value[192:] - high)
                main[part, :, where] = main[part, :, where] + kept
                edge[part, :, where] = edge[part, :, where] + rows(low, high)


CHUNKS = ((0, 64), (192, 64), (64, 128))


def step_kernel(
    n_row, n_col,
    object_hbm, probe_hbm, intensity_hbm, offsets_hbm, counts_hbm, tab_hbm, order_hbm,
    out_ref,
    core, probe, measured, tab, order, offsets, counts,
    pack, got, ends, corner_got, side, corner, rolled, scaled,
    core_sum, side_sum, ends_sum, corner_sum,
    back_pack, back_got, back_ends, back_corner,
    load_sem, send_sem, recv_sem,
):
    r, c = lax.axis_index("row"), lax.axis_index("col")
    has = {"left": c > 0, "right": c < n_col - 1, "up": r > 0, "down": r < n_row - 1}
    where = {"left": (r, c - 1), "right": (r, c + 1), "up": (r - 1, c), "down": (r + 1, c)}
    opposite = {"left": "right", "right": "left", "up": "down", "down": "up"}

    barrier = pltpu.get_barrier_semaphore()
    for way in where:
        @pl.when(has[way])
        def _():
            pl.semaphore_signal(barrier, inc=1, device_id=where[way], device_id_type=MESH)

    loads = [
        pltpu.make_async_copy(source, target, load_sem.at[at])
        for at, (source, target) in enumerate((
            (object_hbm, core), (offsets_hbm, offsets), (counts_hbm, counts), (probe_hbm, probe),
            (intensity_hbm, measured), (order_hbm, order), (tab_hbm, tab),
        ))
    ]
    for load in loads:
        load.start()

    def copy(at, way, source, target):
        return pltpu.make_async_remote_copy(
            src_ref=source, dst_ref=target, send_sem=send_sem.at[at], recv_sem=recv_sem.at[at],
            device_id=where[way], device_id_type=MESH,
        )

    sent = []

    def send(at, way, source, target):
        made = copy(at, way, source, target)
        sent.append((way, made))

        @pl.when(has[way])
        def _():
            made.start()

        return made

    def receive(way, made):
        @pl.when(has[opposite[way]])
        def _():
            made.wait_recv()

    zeros = jnp.zeros
    for way, spots in {
        "right": ((got, 0), (back_got, 1)),
        "left": ((got, 1), (back_got, 0)),
    }.items():
        @pl.when(jnp.logical_not(has[way]))
        def _():
            for ref, at in spots:
                ref[at] = zeros(ref.shape[1:], f32)
    for way, at in (("down", 0), ("up", 64)):
        @pl.when(jnp.logical_not(has[way]))
        def _():
            for ref in (ends, corner_got):
                ref[:, at : at + 64, :] = zeros((2, 64, ref.shape[2]), f32)
    for way, at in (("up", 0), ("down", 64)):
        @pl.when(jnp.logical_not(has[way]))
        def _():
            for ref in (back_ends, back_corner):
                ref[:, at : at + 64, :] = zeros((2, 64, ref.shape[2]), f32)
    for ref in (core_sum, side_sum, ends_sum, corner_sum):
        ref[...] = jnp.zeros_like(ref)

    first_half = lax.broadcasted_iota(jnp.int32, (1, HALF), 1) < MARGIN

    def turned(value):
        return pltpu.roll(value, MARGIN, 1)

    loads[0].wait()
    pack[0] = jnp.where(first_half, core[0, :, :HALF], turned(core[1, :, :HALF]))
    pack[1] = jnp.where(first_half, turned(core[0, :, HALF:]), core[1, :, HALF:])

    peers = sum(jnp.where(has[way], 1, 0) for way in where)
    pl.semaphore_wait(barrier, peers)

    at = 0
    fore = {}
    for start, size in CHUNKS:
        for slot, way in ((0, "left"), (1, "right")):
            part = pl.ds(start, size)
            fore[start, way] = send(at, way, pack.at[slot, part], got.at[slot, part])
            at += 1
    ends_up = send(at, "up", core.at[:, pl.ds(0, 64)], ends.at[:, pl.ds(0, 64)])
    ends_down = send(at + 1, "down", core.at[:, pl.ds(192, 64)], ends.at[:, pl.ds(64, 64)])
    at += 2

    for load in loads[1:]:
        load.wait()
    for number in range(4):
        prepare_probe(probe, rolled, number, offsets[0, number] - MARGIN, offsets[1, number] - MARGIN)
    for number in range(4):
        prepare_intensity(measured, order, scaled, number)

    for way in ("left", "right"):
        receive(way, fore[0, way])
    corner_up = send(at, "up", got.at[:, pl.ds(0, 64)], corner_got.at[:, pl.ds(0, 64)])
    for way in ("left", "right"):
        receive(way, fore[192, way])
    corner_down = send(at + 1, "down", got.at[:, pl.ds(192, 64)], corner_got.at[:, pl.ds(64, 64)])
    at += 2
    for way in ("left", "right"):
        receive(way, fore[64, way])
    side[0] = jnp.where(first_half, got[0], turned(got[1]))
    side[1] = jnp.where(first_half, turned(got[0]), got[1])
    receive("up", ends_up)
    receive("down", ends_down)
    receive("up", corner_up)
    receive("down", corner_down)
    corner[0] = jnp.where(first_half, corner_got[0], turned(corner_got[1]))
    corner[1] = jnp.where(first_half, turned(corner_got[0]), corner_got[1])

    @pl.loop(0, 4)
    def _(number):
        valid = jnp.where(number < counts[0, 0], 1.0, 0.0)
        one_view(
            number, offsets[0, number] - MARGIN, offsets[1, number] - MARGIN, valid, core, side, ends, corner,
            rolled, scaled, tab, (core_sum, side_sum, ends_sum, corner_sum),
        )

    grads = []
    for way, start in (("down", 0), ("up", 64)):
        part = pl.ds(start, 64)
        grads.append((way, start, send(at, way, corner_sum.at[:, part], back_corner.at[:, part])))
        at += 1
    back = {}

    def pack_sides(start, size):
        part = slice(start, start + size)
        re, im = side_sum[0, part], side_sum[1, part]
        back_pack[0, part] = jnp.where(first_half, re, turned(im))
        back_pack[1, part] = jnp.where(first_half, turned(re), im)

    def send_sides(start, size):
        nonlocal at
        part = pl.ds(start, size)
        for slot, way in ((0, "right"), (1, "left")):
            back[start, way] = send(at, way, back_pack.at[slot, part], back_got.at[slot, part])
            at += 1

    pack_sides(64, 128)
    send_sides(64, 128)
    edge = []
    for way, start in (("down", 0), ("up", 64)):
        part = pl.ds(start, 64)
        edge.append((way, start, send(at, way, ends_sum.at[:, part], back_ends.at[:, part])))
        at += 1
    for way, start, made in grads:
        receive(way, made)
        begin = 0 if start == 0 else 192
        side_sum[:, begin : begin + 64] = side_sum[:, begin : begin + 64] + back_corner[:, start : start + 64]
        pack_sides(begin, 64)
        send_sides(begin, 64)
    for way, start, made in edge:
        receive(way, made)
        begin = 0 if start == 0 else 192
        core_sum[:, begin : begin + 64] = core_sum[:, begin : begin + 64] + back_ends[:, start : start + 64]
    out_ref[...] = core[...] - step_size * core_sum[...]
    for start, size in ((64, 128), (0, 64), (192, 64)):
        part = slice(start, start + size)
        for way in ("right", "left"):
            receive(way, back[start, way])
        from_left, from_right = back_got[0, part], back_got[1, part]
        for at_part, left_part, right_part in (
            (0, from_left, turned(from_right)),
            (1, turned(from_left), from_right),
        ):
            out_ref[at_part, part, :HALF] = out_ref[at_part, part, :HALF] - step_size * jnp.where(first_half, left_part, 0.0)
            out_ref[at_part, part, HALF:] = out_ref[at_part, part, HALF:] - step_size * jnp.where(first_half, 0.0, right_part)
    for way, made in sent:
        @pl.when(has[way])
        def _():
            made.wait_send()


def per_device(n_row, n_col, object_field, probe_field, intensity, view_offsets, view_counts):
    anywhere = pl.BlockSpec(memory_space=pl.ANY)
    vmem = pltpu.VMEM
    n_copies = 20
    return pl.pallas_call(
        functools.partial(step_kernel, n_row, n_col),
        out_shape=jax.ShapeDtypeStruct(object_field.shape, f32),
        in_specs=[anywhere] * 7,
        out_specs=pl.BlockSpec(memory_space=vmem),
        scratch_shapes=[
            vmem((2, 256, 256), f32), vmem((2, 256, 256), f32), vmem((4, 256, 256), f32),
            vmem((2, 2, 2, 256, 256), bf16), vmem((2, 256, 256), bf16),
            pltpu.SMEM((2, 4), jnp.int32), pltpu.SMEM((1, 1), jnp.int32),
            vmem((2, 256, 128), f32), vmem((2, 256, 128), f32), vmem((2, 128, 256), f32), vmem((2, 128, 128), f32),
            vmem((2, 256, 128), f32), vmem((2, 128, 128), f32),
            vmem((4, 2, 256, 256), f32), vmem((4, 2, 128, 256), f32),
            vmem((2, 256, 256), f32), vmem((2, 256, 128), f32), vmem((2, 128, 256), f32), vmem((2, 128, 128), f32),
            vmem((2, 256, 128), f32), vmem((2, 256, 128), f32), vmem((2, 128, 256), f32), vmem((2, 128, 128), f32),
            pltpu.SemaphoreType.DMA((7,)), pltpu.SemaphoreType.DMA((n_copies,)), pltpu.SemaphoreType.DMA((n_copies,)),
        ],
        compiler_params=pltpu.CompilerParams(
            collective_id=0, has_side_effects=True, vmem_limit_bytes=56 * 2**20
        ),
    )(
        object_field, probe_field, intensity[0, 0], view_offsets[0, 0].T, view_counts,
        jnp.asarray(dft_tables()), jnp.asarray(order_tables()),
    )


def solution(mesh):
    in_specs = (
        P(None, "row", "col"),
        P(),
        P("row", "col", None, None, None),
        P("row", "col", None, None),
        P("row", "col"),
    )
    out_specs = P(None, "row", "col")
    body = functools.partial(per_device, mesh.shape["row"], mesh.shape["col"])
    return jax.shard_map(body, mesh=mesh, in_specs=in_specs, out_specs=out_specs, check_vma=False)
```

```python
import functools

import jax
import jax.numpy as jnp
import ml_dtypes
import numpy as np
from jax import lax
from jax.experimental import pallas as pl
from jax.experimental.pallas import tpu as pltpu
from jax.sharding import PartitionSpec as P

MESH = pl.DeviceIdType.MESH
CORE = 256
MARGIN = 64
HALF = 128
smooth_eps = 0.1
step_size = 0.2
f32, bf16 = jnp.float32, jnp.bfloat16


def dft_tables():
    index = np.arange(HALF)
    forms = []
    for parity in (0, 1):
        turns = (index[:, None] * (2 * index[None, :] + parity)) % CORE
        entries = np.exp(-2j * np.pi * turns / CORE) / np.sqrt(CORE)
        forms.append(np.block([[entries.real, entries.imag], [-entries.imag, entries.real]]))
    forms = np.stack(forms).astype(np.float32)
    forms = np.stack([forms, np.swapaxes(forms, 1, 2)])
    high = forms.astype(ml_dtypes.bfloat16)
    low = (forms - high.astype(np.float32)).astype(ml_dtypes.bfloat16)
    return np.stack([high, low], axis=2).reshape(8, CORE, CORE)


def order_tables():
    move = np.zeros((CORE, CORE), np.float32)
    index = np.arange(HALF)
    move[2 * index, index] = 1.0
    move[2 * index + 1, HALF + index] = 1.0
    return np.stack([move, move.T]).astype(ml_dtypes.bfloat16)


def table(tab, form, parity, low):
    return tab[4 * form + 2 * parity + low]


def dot(left, right):
    return jnp.dot(left, right, preferred_element_type=f32)


def split(value):
    high = value.astype(bf16)
    return high, (value - high.astype(f32)).astype(bf16)


def times_table(value, tab, form, parity):
    high, low = split(value)
    t_high, t_low = table(tab, form, parity, 0), table(tab, form, parity, 1)
    return dot(high, t_high) + dot(low, t_high) + dot(high, t_low)


def table_times(value, tab, form, parity):
    high, low = split(value)
    t_high, t_low = table(tab, form, parity, 0), table(tab, form, parity, 1)
    return dot(t_high, high) + dot(t_high, low) + dot(t_low, high)


def lanes(*parts):
    return jnp.concatenate(parts, axis=1)


def rows(*parts):
    return jnp.concatenate(parts, axis=0)


def columns(tile):
    return slice(HALF * tile, HALF * tile + HALF)


def prepare_intensity(measured, tab, scaled, number):
    right, left = tab[8], tab[9]
    value = measured[number]
    first = value.astype(bf16)
    rest = value - first.astype(f32)
    second = rest.astype(bf16)
    third = (rest - second.astype(f32)).astype(bf16)
    moved = [dot(left, dot(part, right).astype(bf16)) for part in (first, second, third)]
    total = (moved[0] + moved[1] + moved[2]) + smooth_eps
    scaled[number, 0] = total[:HALF]
    scaled[number, 1] = total[HALF:]


def prepare_probe(probe, rolled, number, row_off, col_off):
    for part in range(2):
        turned = pltpu.roll(probe[part], lax.rem(row_off + CORE, CORE), 0)
        rolled[number, part] = pltpu.roll(turned, lax.rem(col_off + CORE, CORE), 1)


def one_view(number, row_off, col_off, valid, core, side, ends, corner, rolled, scaled, tab, sums):
    lane = lax.broadcasted_iota(jnp.int32, (1, HALF), 1)
    line = lax.broadcasted_iota(jnp.int32, (MARGIN, 1), 0)
    in_side = (lane < col_off, lane >= HALF + col_off)
    in_low, in_high = line < row_off, line >= MARGIN + row_off

    def patch(part, tile):
        middle = jnp.where(in_side[tile], side[part], core[part, :, columns(tile)])
        outer = jnp.where(in_side[tile], corner[part], ends[part, :, columns(tile)])
        low = jnp.where(in_low, outer[:64], middle[:64])
        high = jnp.where(in_high, outer[64:], middle[192:])
        return rows(low, middle[64:192], high)

    waves = []
    for tile in range(2):
        p_re, p_im = rolled[number, 0, :, columns(tile)], rolled[number, 1, :, columns(tile)]
        o_re, o_im = patch(0, tile), patch(1, tile)
        waves.append(lanes(p_re * o_re - p_im * o_im, p_re * o_im + p_im * o_re))
    yield
    even = times_table(waves[0] + waves[1], tab, 0, 0)
    odd = times_table(waves[0] - waves[1], tab, 0, 1)
    yield

    def stacked(even_cols, odd_cols):
        return rows(
            lanes(even_cols[:, :HALF], odd_cols[:, :HALF]),
            lanes(even_cols[:, HALF:], odd_cols[:, HALF:]),
        )

    halves = (
        stacked(even[:HALF] + even[HALF:], odd[:HALF] + odd[HALF:]),
        stacked(even[:HALF] - even[HALF:], odd[:HALF] - odd[HALF:]),
    )
    fars = [table_times(halves[parity], tab, 1, parity) for parity in range(2)]
    yield
    back = []
    for parity, far in enumerate(fars):
        far_re, far_im = far[:HALF], far[HALF:]
        wanted = scaled[number, parity]
        found = far_re * far_re + far_im * far_im + smooth_eps
        scaling = 1.0 - wanted * lax.rsqrt(wanted * found)
        corrected = rows(far_re * scaling, far_im * scaling)
        back.append(table_times(corrected, tab, 0, parity))
    yield
    upper, lower = back[0] + back[1], back[0] - back[1]
    re = rows(upper[:HALF], lower[:HALF])
    im = rows(upper[HALF:], lower[HALF:])
    even = times_table(lanes(re[:, :HALF], im[:, :HALF]), tab, 1, 0)
    odd = times_table(lanes(re[:, HALF:], im[:, HALF:]), tab, 1, 1)
    yield
    core_sum, side_sum, ends_sum, corner_sum = sums
    for tile, wave in ((0, even + odd), (1, even - odd)):
        b_re, b_im = wave[:, :HALF], wave[:, HALF:]
        p_re, p_im = rolled[number, 0, :, columns(tile)], rolled[number, 1, :, columns(tile)]
        for part, raw in ((0, p_re * b_re + p_im * b_im), (1, p_re * b_im - p_im * b_re)):
            grad = raw * valid
            outside = jnp.where(in_side[tile], grad, 0.0)
            for value, main, edge, where in (
                (grad - outside, core_sum, ends_sum, columns(tile)),
                (outside, side_sum, corner_sum, slice(0, HALF)),
            ):
                low = jnp.where(in_low, value[:64], 0.0)
                high = jnp.where(in_high, value[192:], 0.0)
                main[part, :64, where] = main[part, :64, where] + (value[:64] - low)
                main[part, 64:192, where] = main[part, 64:192, where] + value[64:192]
                main[part, 192:, where] = main[part, 192:, where] + (value[192:] - high)
                edge[part, :64, where] = edge[part, :64, where] + low
                edge[part, 64:, where] = edge[part, 64:, where] + high
    yield


CHUNKS = ((0, 64), (192, 64), (64, 128))


def step_kernel(
    n_row, n_col,
    object_hbm, probe_hbm, intensity_hbm, offsets_hbm, counts_hbm, tab_hbm,
    out_ref,
    core, probe, measured, tab, offsets, counts,
    pack, got, ends, corner_got, side, corner, rolled, scaled,
    core_sum, side_sum, ends_sum, corner_sum,
    back_pack, back_got, back_ends, back_corner,
    load_sem, send_sem, recv_sem,
):
    r, c = lax.axis_index("row"), lax.axis_index("col")
    has = {"left": c > 0, "right": c < n_col - 1, "up": r > 0, "down": r < n_row - 1}
    where = {"left": (r, c - 1), "right": (r, c + 1), "up": (r - 1, c), "down": (r + 1, c)}
    opposite = {"left": "right", "right": "left", "up": "down", "down": "up"}

    barrier = pltpu.get_barrier_semaphore()
    for way in where:
        @pl.when(has[way])
        def _():
            pl.semaphore_signal(barrier, inc=1, device_id=where[way], device_id_type=MESH)

    loads = [
        pltpu.make_async_copy(source, target, load_sem.at[at])
        for at, (source, target) in enumerate((
            (object_hbm, core), (offsets_hbm, offsets), (counts_hbm, counts), (probe_hbm, probe),
            (intensity_hbm, measured), (tab_hbm, tab),
        ))
    ]
    for load in loads:
        load.start()

    def copy(at, way, source, target):
        return pltpu.make_async_remote_copy(
            src_ref=source, dst_ref=target, send_sem=send_sem.at[at], recv_sem=recv_sem.at[at],
            device_id=where[way], device_id_type=MESH,
        )

    sent = []

    def send(at, way, source, target):
        made = copy(at, way, source, target)
        sent.append((way, made))

        @pl.when(has[way])
        def _():
            made.start()

        return made

    def receive(way, made):
        @pl.when(has[opposite[way]])
        def _():
            made.wait_recv()

    zeros = jnp.zeros
    for way, spots in {
        "right": ((got, 0), (back_got, 1)),
        "left": ((got, 1), (back_got, 0)),
    }.items():
        @pl.when(jnp.logical_not(has[way]))
        def _():
            for ref, at in spots:
                ref[at] = zeros(ref.shape[1:], f32)
    for way, at in (("down", 0), ("up", 64)):
        @pl.when(jnp.logical_not(has[way]))
        def _():
            for ref in (ends, corner_got):
                ref[:, at : at + 64, :] = zeros((2, 64, ref.shape[2]), f32)
    for way, at in (("up", 0), ("down", 64)):
        @pl.when(jnp.logical_not(has[way]))
        def _():
            for ref in (back_ends, back_corner):
                ref[:, at : at + 64, :] = zeros((2, 64, ref.shape[2]), f32)
    for ref in (core_sum, side_sum, ends_sum, corner_sum):
        ref[...] = jnp.zeros_like(ref)

    first_half = lax.broadcasted_iota(jnp.int32, (1, HALF), 1) < MARGIN

    def turned(value):
        return pltpu.roll(value, MARGIN, 1)

    loads[0].wait()
    pack[0] = jnp.where(first_half, core[0, :, :HALF], turned(core[1, :, :HALF]))
    pack[1] = jnp.where(first_half, turned(core[0, :, HALF:]), core[1, :, HALF:])

    peers = sum(jnp.where(has[way], 1, 0) for way in where)
    pl.semaphore_wait(barrier, peers)

    at = 0
    fore = {}
    for start, size in CHUNKS:
        for slot, way in ((0, "left"), (1, "right")):
            part = pl.ds(start, size)
            fore[start, way] = send(at, way, pack.at[slot, part], got.at[slot, part])
            at += 1
    ends_up = send(at, "up", core.at[:, pl.ds(0, 64)], ends.at[:, pl.ds(0, 64)])
    ends_down = send(at + 1, "down", core.at[:, pl.ds(192, 64)], ends.at[:, pl.ds(64, 64)])
    at += 2

    for load in loads[1:]:
        load.wait()
    for number in range(4):
        prepare_probe(probe, rolled, number, offsets[0, number] - MARGIN, offsets[1, number] - MARGIN)
    for number in range(4):
        prepare_intensity(measured, tab, scaled, number)

    for way in ("left", "right"):
        receive(way, fore[0, way])
    corner_up = send(at, "up", got.at[:, pl.ds(0, 64)], corner_got.at[:, pl.ds(0, 64)])
    for way in ("left", "right"):
        receive(way, fore[192, way])
    corner_down = send(at + 1, "down", got.at[:, pl.ds(192, 64)], corner_got.at[:, pl.ds(64, 64)])
    at += 2
    for way in ("left", "right"):
        receive(way, fore[64, way])
    side[0] = jnp.where(first_half, got[0], turned(got[1]))
    side[1] = jnp.where(first_half, turned(got[0]), got[1])
    receive("up", ends_up)
    receive("down", ends_down)
    receive("up", corner_up)
    receive("down", corner_down)
    corner[0] = jnp.where(first_half, corner_got[0], turned(corner_got[1]))
    corner[1] = jnp.where(first_half, turned(corner_got[0]), corner_got[1])

    def view(number):
        valid = jnp.where(number < counts[0, 0], 1.0, 0.0)
        return one_view(
            number, offsets[0, number] - MARGIN, offsets[1, number] - MARGIN, valid, core, side, ends, corner,
            rolled, scaled, tab, (core_sum, side_sum, ends_sum, corner_sum),
        )

    @pl.loop(0, 2)
    def _(pair):
        for _ in zip(view(2 * pair), view(2 * pair + 1)):
            pass

    grads = []
    for way, start in (("down", 0), ("up", 64)):
        part = pl.ds(start, 64)
        grads.append((way, start, send(at, way, corner_sum.at[:, part], back_corner.at[:, part])))
        at += 1
    back = {}

    def pack_sides(start, size):
        part = slice(start, start + size)
        re, im = side_sum[0, part], side_sum[1, part]
        back_pack[0, part] = jnp.where(first_half, re, turned(im))
        back_pack[1, part] = jnp.where(first_half, turned(re), im)

    def send_sides(start, size):
        nonlocal at
        part = pl.ds(start, size)
        for slot, way in ((0, "right"), (1, "left")):
            back[start, way] = send(at, way, back_pack.at[slot, part], back_got.at[slot, part])
            at += 1

    pack_sides(64, 128)
    send_sides(64, 128)
    edge = []
    for way, start in (("down", 0), ("up", 64)):
        part = pl.ds(start, 64)
        edge.append((way, start, send(at, way, ends_sum.at[:, part], back_ends.at[:, part])))
        at += 1
    for way, start, made in grads:
        receive(way, made)
        begin = 0 if start == 0 else 192
        side_sum[:, begin : begin + 64] = side_sum[:, begin : begin + 64] + back_corner[:, start : start + 64]
        pack_sides(begin, 64)
        send_sides(begin, 64)
    for way, start, made in edge:
        receive(way, made)
        begin = 0 if start == 0 else 192
        core_sum[:, begin : begin + 64] = core_sum[:, begin : begin + 64] + back_ends[:, start : start + 64]
    out_ref[...] = core[...] - step_size * core_sum[...]
    for start, size in ((64, 128), (0, 64), (192, 64)):
        part = slice(start, start + size)
        for way in ("right", "left"):
            receive(way, back[start, way])
        from_left, from_right = back_got[0, part], back_got[1, part]
        for at_part, left_part, right_part in (
            (0, from_left, turned(from_right)),
            (1, turned(from_left), from_right),
        ):
            out_ref[at_part, part, :HALF] = out_ref[at_part, part, :HALF] - step_size * jnp.where(first_half, left_part, 0.0)
            out_ref[at_part, part, HALF:] = out_ref[at_part, part, HALF:] - step_size * jnp.where(first_half, 0.0, right_part)
    for way, made in sent:
        @pl.when(has[way])
        def _():
            made.wait_send()


def per_device(n_row, n_col, object_field, probe_field, intensity, view_offsets, view_counts):
    anywhere = pl.BlockSpec(memory_space=pl.ANY)
    vmem = pltpu.VMEM
    n_copies = 20
    return pl.pallas_call(
        functools.partial(step_kernel, n_row, n_col),
        out_shape=jax.ShapeDtypeStruct(object_field.shape, f32),
        in_specs=[anywhere] * 6,
        out_specs=pl.BlockSpec(memory_space=vmem),
        scratch_shapes=[
            vmem((2, 256, 256), f32), vmem((2, 256, 256), f32), vmem((4, 256, 256), f32),
            vmem((10, 256, 256), bf16),
            pltpu.SMEM((2, 4), jnp.int32), pltpu.SMEM((1, 1), jnp.int32),
            vmem((2, 256, 128), f32), vmem((2, 256, 128), f32), vmem((2, 128, 256), f32), vmem((2, 128, 128), f32),
            vmem((2, 256, 128), f32), vmem((2, 128, 128), f32),
            vmem((4, 2, 256, 256), f32), vmem((4, 2, 128, 256), f32),
            vmem((2, 256, 256), f32), vmem((2, 256, 128), f32), vmem((2, 128, 256), f32), vmem((2, 128, 128), f32),
            vmem((2, 256, 128), f32), vmem((2, 256, 128), f32), vmem((2, 128, 256), f32), vmem((2, 128, 128), f32),
            pltpu.SemaphoreType.DMA((6,)), pltpu.SemaphoreType.DMA((n_copies,)), pltpu.SemaphoreType.DMA((n_copies,)),
        ],
        compiler_params=pltpu.CompilerParams(
            collective_id=0, has_side_effects=True, vmem_limit_bytes=55574528
        ),
    )(
        object_field, probe_field, intensity[0, 0], view_offsets[0, 0].T, view_counts,
        jnp.asarray(np.concatenate([dft_tables(), order_tables()])),
    )


def solution(mesh):
    in_specs = (
        P(None, "row", "col"),
        P(),
        P("row", "col", None, None, None),
        P("row", "col", None, None),
        P("row", "col"),
    )
    out_specs = P(None, "row", "col")
    body = functools.partial(per_device, mesh.shape["row"], mesh.shape["col"])
    return jax.shard_map(body, mesh=mesh, in_specs=in_specs, out_specs=out_specs, check_vma=False)
```

```python
import functools

import jax
import jax.numpy as jnp
import ml_dtypes
import numpy as np
from jax import lax
from jax.experimental import pallas as pl
from jax.experimental.pallas import tpu as pltpu
from jax.sharding import PartitionSpec as P

MESH = pl.DeviceIdType.MESH
CORE = 256
MARGIN = 64
HALF = 128
smooth_eps = 0.1
step_size = 0.2
f32, bf16 = jnp.float32, jnp.bfloat16


def dft_tables():
    index = np.arange(HALF)
    forms = []
    for parity in (0, 1):
        turns = (index[:, None] * (2 * index[None, :] + parity)) % CORE
        entries = np.exp(-2j * np.pi * turns / CORE) / np.sqrt(CORE)
        forms.append(np.block([[entries.real, entries.imag], [-entries.imag, entries.real]]))
    forms = np.stack(forms).astype(np.float32)
    forms = np.stack([forms, np.swapaxes(forms, 1, 2)])
    high = forms.astype(ml_dtypes.bfloat16)
    low = (forms - high.astype(np.float32)).astype(ml_dtypes.bfloat16)
    return np.stack([high, low], axis=2).reshape(8, CORE, CORE)


def order_tables():
    move = np.zeros((CORE, CORE), np.float32)
    index = np.arange(HALF)
    move[2 * index, index] = 1.0
    move[2 * index + 1, HALF + index] = 1.0
    return np.stack([move, move.T]).astype(ml_dtypes.bfloat16)


def table(tab, form, parity, low):
    return tab[4 * form + 2 * parity + low]


def dot(left, right):
    return jnp.dot(left, right, preferred_element_type=f32)


def split(value):
    high = value.astype(bf16)
    return high, (value - high.astype(f32)).astype(bf16)


def times_table(value, tab, form, parity):
    high, low = split(value)
    t_high, t_low = table(tab, form, parity, 0), table(tab, form, parity, 1)
    return dot(high, t_high) + dot(low, t_high) + dot(high, t_low)


def table_times(value, tab, form, parity):
    high, low = split(value)
    t_high, t_low = table(tab, form, parity, 0), table(tab, form, parity, 1)
    return dot(t_high, high) + dot(t_high, low) + dot(t_low, high)


def lanes(*parts):
    return jnp.concatenate(parts, axis=1)


def rows(*parts):
    return jnp.concatenate(parts, axis=0)


def columns(tile):
    return slice(HALF * tile, HALF * tile + HALF)


def prepare_intensity(measured, tab, scaled, number):
    right, left = tab[8], tab[9]
    value = measured[number]
    first = value.astype(bf16)
    rest = value - first.astype(f32)
    second = rest.astype(bf16)
    third = (rest - second.astype(f32)).astype(bf16)
    moved = [dot(left, dot(part, right).astype(bf16)) for part in (first, second, third)]
    total = (moved[0] + moved[1] + moved[2]) + smooth_eps
    scaled[number, 0] = total[:HALF]
    scaled[number, 1] = total[HALF:]


def prepare_probe(probe, rolled, number, row_off, col_off):
    for part in range(2):
        turned = pltpu.roll(probe[part], lax.rem(row_off + CORE, CORE), 0)
        rolled[number, part] = pltpu.roll(turned, lax.rem(col_off + CORE, CORE), 1)


def one_view(number, row_off, col_off, valid, core, side, ends, corner, rolled, scaled, tab, sums):
    lane = lax.broadcasted_iota(jnp.int32, (1, HALF), 1)
    line = lax.broadcasted_iota(jnp.int32, (MARGIN, 1), 0)
    in_side = (lane < col_off, lane >= HALF + col_off)
    in_low, in_high = line < row_off, line >= MARGIN + row_off

    def patch(part, tile):
        middle = jnp.where(in_side[tile], side[part], core[part, :, columns(tile)])
        outer = jnp.where(in_side[tile], corner[part], ends[part, :, columns(tile)])
        low = jnp.where(in_low, outer[:64], middle[:64])
        high = jnp.where(in_high, outer[64:], middle[192:])
        return rows(low, middle[64:192], high)

    waves = []
    for tile in range(2):
        p_re, p_im = rolled[number, 0, :, columns(tile)], rolled[number, 1, :, columns(tile)]
        o_re, o_im = patch(0, tile), patch(1, tile)
        waves.append(lanes(p_re * o_re - p_im * o_im, p_re * o_im + p_im * o_re))
    yield
    even = times_table(waves[0] + waves[1], tab, 0, 0)
    odd = times_table(waves[0] - waves[1], tab, 0, 1)
    yield

    def stacked(even_cols, odd_cols):
        return rows(
            lanes(even_cols[:, :HALF], odd_cols[:, :HALF]),
            lanes(even_cols[:, HALF:], odd_cols[:, HALF:]),
        )

    halves = (
        stacked(even[:HALF] + even[HALF:], odd[:HALF] + odd[HALF:]),
        stacked(even[:HALF] - even[HALF:], odd[:HALF] - odd[HALF:]),
    )
    fars = [table_times(halves[parity], tab, 1, parity) for parity in range(2)]
    yield
    back = []
    for parity, far in enumerate(fars):
        far_re, far_im = far[:HALF], far[HALF:]
        wanted = scaled[number, parity]
        found = far_re * far_re + far_im * far_im + smooth_eps
        scaling = 1.0 - wanted * lax.rsqrt(wanted * found)
        corrected = rows(far_re * scaling, far_im * scaling)
        back.append(table_times(corrected, tab, 0, parity))
    yield
    upper, lower = back[0] + back[1], back[0] - back[1]
    re = rows(upper[:HALF], lower[:HALF])
    im = rows(upper[HALF:], lower[HALF:])
    even = times_table(lanes(re[:, :HALF], im[:, :HALF]), tab, 1, 0)
    odd = times_table(lanes(re[:, HALF:], im[:, HALF:]), tab, 1, 1)
    yield
    core_sum, side_sum, ends_sum, corner_sum = sums
    for tile, wave in ((0, even + odd), (1, even - odd)):
        b_re, b_im = wave[:, :HALF], wave[:, HALF:]
        p_re, p_im = rolled[number, 0, :, columns(tile)], rolled[number, 1, :, columns(tile)]
        for part, raw in ((0, p_re * b_re + p_im * b_im), (1, p_re * b_im - p_im * b_re)):
            grad = raw * valid
            outside = jnp.where(in_side[tile], grad, 0.0)
            for value, main, edge, where in (
                (grad - outside, core_sum, ends_sum, columns(tile)),
                (outside, side_sum, corner_sum, slice(0, HALF)),
            ):
                low = jnp.where(in_low, value[:64], 0.0)
                high = jnp.where(in_high, value[192:], 0.0)
                main[part, :64, where] = main[part, :64, where] + (value[:64] - low)
                main[part, 64:192, where] = main[part, 64:192, where] + value[64:192]
                main[part, 192:, where] = main[part, 192:, where] + (value[192:] - high)
                edge[part, :64, where] = edge[part, :64, where] + low
                edge[part, 64:, where] = edge[part, 64:, where] + high
    yield


CHUNKS = ((0, 64), (192, 64), (64, 128))


def step_kernel(
    n_row, n_col,
    object_hbm, probe_hbm, intensity_hbm, offsets_hbm, counts_hbm, tab_hbm,
    out_ref,
    core, probe, measured, tab, offsets, counts,
    pack, got, ends, corner_got, side, corner, rolled, scaled,
    core_sum, side_sum, ends_sum, corner_sum,
    back_pack, back_got, back_ends, back_corner,
    load_sem, send_sem, recv_sem,
):
    r, c = lax.axis_index("row"), lax.axis_index("col")
    has = {"left": c > 0, "right": c < n_col - 1, "up": r > 0, "down": r < n_row - 1}
    where = {"left": (r, c - 1), "right": (r, c + 1), "up": (r - 1, c), "down": (r + 1, c)}
    opposite = {"left": "right", "right": "left", "up": "down", "down": "up"}

    barrier = pltpu.get_barrier_semaphore()
    for way in where:
        @pl.when(has[way])
        def _():
            pl.semaphore_signal(barrier, inc=1, device_id=where[way], device_id_type=MESH)

    loads = [
        pltpu.make_async_copy(source, target, load_sem.at[at])
        for at, (source, target) in enumerate((
            (object_hbm, core), (offsets_hbm, offsets), (counts_hbm, counts), (probe_hbm, probe),
            (intensity_hbm, measured), (tab_hbm, tab),
        ))
    ]
    for load in loads:
        load.start()

    def copy(at, way, source, target):
        return pltpu.make_async_remote_copy(
            src_ref=source, dst_ref=target, send_sem=send_sem.at[at], recv_sem=recv_sem.at[at],
            device_id=where[way], device_id_type=MESH,
        )

    sent = []

    def send(at, way, source, target):
        made = copy(at, way, source, target)
        sent.append((way, made))

        @pl.when(has[way])
        def _():
            made.start()

        return made

    def receive(way, made):
        @pl.when(has[opposite[way]])
        def _():
            made.wait_recv()

    zeros = jnp.zeros
    for way, spots in {
        "right": ((got, 0), (back_got, 1)),
        "left": ((got, 1), (back_got, 0)),
    }.items():
        @pl.when(jnp.logical_not(has[way]))
        def _():
            for ref, at in spots:
                ref[at] = zeros(ref.shape[1:], f32)
    for way, at in (("down", 0), ("up", 64)):
        @pl.when(jnp.logical_not(has[way]))
        def _():
            for ref in (ends, corner_got):
                ref[:, at : at + 64, :] = zeros((2, 64, ref.shape[2]), f32)
    for way, at in (("up", 0), ("down", 64)):
        @pl.when(jnp.logical_not(has[way]))
        def _():
            for ref in (back_ends, back_corner):
                ref[:, at : at + 64, :] = zeros((2, 64, ref.shape[2]), f32)
    for ref in (core_sum, side_sum, ends_sum, corner_sum):
        ref[...] = jnp.zeros_like(ref)

    first_half = lax.broadcasted_iota(jnp.int32, (1, HALF), 1) < MARGIN

    def turned(value):
        return pltpu.roll(value, MARGIN, 1)

    loads[0].wait()
    pack[0] = jnp.where(first_half, core[0, :, :HALF], turned(core[1, :, :HALF]))
    pack[1] = jnp.where(first_half, turned(core[0, :, HALF:]), core[1, :, HALF:])

    peers = sum(jnp.where(has[way], 1, 0) for way in where)
    pl.semaphore_wait(barrier, peers)

    at = 0
    fore = {}
    for start, size in CHUNKS:
        for slot, way in ((0, "left"), (1, "right")):
            part = pl.ds(start, size)
            fore[start, way] = send(at, way, pack.at[slot, part], got.at[slot, part])
            at += 1
    ends_up = send(at, "up", core.at[:, pl.ds(0, 64)], ends.at[:, pl.ds(0, 64)])
    ends_down = send(at + 1, "down", core.at[:, pl.ds(192, 64)], ends.at[:, pl.ds(64, 64)])
    at += 2

    for load in loads[1:]:
        load.wait()
    for number in range(4):
        prepare_probe(probe, rolled, number, offsets[0, number] - MARGIN, offsets[1, number] - MARGIN)
    for number in range(4):
        prepare_intensity(measured, tab, scaled, number)

    for way in ("left", "right"):
        receive(way, fore[0, way])
    corner_up = send(at, "up", got.at[:, pl.ds(0, 64)], corner_got.at[:, pl.ds(0, 64)])
    for way in ("left", "right"):
        receive(way, fore[192, way])
    corner_down = send(at + 1, "down", got.at[:, pl.ds(192, 64)], corner_got.at[:, pl.ds(64, 64)])
    at += 2
    for way in ("left", "right"):
        receive(way, fore[64, way])
    side[0] = jnp.where(first_half, got[0], turned(got[1]))
    side[1] = jnp.where(first_half, turned(got[0]), got[1])
    receive("up", ends_up)
    receive("down", ends_down)
    receive("up", corner_up)
    receive("down", corner_down)
    corner[0] = jnp.where(first_half, corner_got[0], turned(corner_got[1]))
    corner[1] = jnp.where(first_half, turned(corner_got[0]), corner_got[1])

    def view(number):
        valid = jnp.where(number < counts[0, 0], 1.0, 0.0)
        return one_view(
            number, offsets[0, number] - MARGIN, offsets[1, number] - MARGIN, valid, core, side, ends, corner,
            rolled, scaled, tab, (core_sum, side_sum, ends_sum, corner_sum),
        )

    @pl.loop(0, 2)
    def _(pair):
        for _ in zip(view(2 * pair), view(2 * pair + 1)):
            pass

    grads = []
    for way, start in (("down", 0), ("up", 64)):
        part = pl.ds(start, 64)
        grads.append((way, start, send(at, way, corner_sum.at[:, part], back_corner.at[:, part])))
        at += 1
    back = {}

    def pack_sides(start, size):
        part = slice(start, start + size)
        re, im = side_sum[0, part], side_sum[1, part]
        back_pack[0, part] = jnp.where(first_half, re, turned(im))
        back_pack[1, part] = jnp.where(first_half, turned(re), im)

    def send_sides(start, size):
        nonlocal at
        part = pl.ds(start, size)
        for slot, way in ((0, "right"), (1, "left")):
            back[start, way] = send(at, way, back_pack.at[slot, part], back_got.at[slot, part])
            at += 1

    pack_sides(64, 128)
    send_sides(64, 128)
    edge = []
    for way, start in (("down", 0), ("up", 64)):
        part = pl.ds(start, 64)
        edge.append((way, start, send(at, way, ends_sum.at[:, part], back_ends.at[:, part])))
        at += 1
    for way, start, made in grads:
        receive(way, made)
        begin = 0 if start == 0 else 192
        side_sum[:, begin : begin + 64] = side_sum[:, begin : begin + 64] + back_corner[:, start : start + 64]
        pack_sides(begin, 64)
        send_sides(begin, 64)
    for way, start, made in edge:
        receive(way, made)
        begin = 0 if start == 0 else 192
        core_sum[:, begin : begin + 64] = core_sum[:, begin : begin + 64] + back_ends[:, start : start + 64]
    out_ref[...] = core[...] - step_size * core_sum[...]
    for start, size in ((64, 128), (0, 64), (192, 64)):
        part = slice(start, start + size)
        for way in ("right", "left"):
            receive(way, back[start, way])
        from_left, from_right = back_got[0, part], back_got[1, part]
        for at_part, left_part, right_part in (
            (0, from_left, turned(from_right)),
            (1, turned(from_left), from_right),
        ):
            out_ref[at_part, part, :HALF] = out_ref[at_part, part, :HALF] - step_size * jnp.where(first_half, left_part, 0.0)
            out_ref[at_part, part, HALF:] = out_ref[at_part, part, HALF:] - step_size * jnp.where(first_half, 0.0, right_part)
    for way, made in sent:
        @pl.when(has[way])
        def _():
            made.wait_send()


def per_device(n_row, n_col, object_field, probe_field, intensity, view_offsets, view_counts):
    anywhere = pl.BlockSpec(memory_space=pl.ANY)
    vmem = pltpu.VMEM
    n_copies = 20
    return pl.pallas_call(
        functools.partial(step_kernel, n_row, n_col),
        out_shape=jax.ShapeDtypeStruct(object_field.shape, f32),
        in_specs=[anywhere] * 6,
        out_specs=pl.BlockSpec(memory_space=vmem),
        scratch_shapes=[
            vmem((2, 256, 256), f32), vmem((2, 256, 256), f32), vmem((4, 256, 256), f32),
            vmem((10, 256, 256), bf16),
            pltpu.SMEM((2, 4), jnp.int32), pltpu.SMEM((1, 1), jnp.int32),
            vmem((2, 256, 128), f32), vmem((2, 256, 128), f32), vmem((2, 128, 256), f32), vmem((2, 128, 128), f32),
            vmem((2, 256, 128), f32), vmem((2, 128, 128), f32),
            vmem((4, 2, 256, 256), f32), vmem((4, 2, 128, 256), f32),
            vmem((2, 256, 256), f32), vmem((2, 256, 128), f32), vmem((2, 128, 256), f32), vmem((2, 128, 128), f32),
            vmem((2, 256, 128), f32), vmem((2, 256, 128), f32), vmem((2, 128, 256), f32), vmem((2, 128, 128), f32),
            pltpu.SemaphoreType.DMA((6,)), pltpu.SemaphoreType.DMA((n_copies,)), pltpu.SemaphoreType.DMA((n_copies,)),
        ],
        compiler_params=pltpu.CompilerParams(
            collective_id=0, has_side_effects=True, vmem_limit_bytes=55574528
        ),
    )(
        object_field, probe_field, intensity[0, 0], pltpu.with_memory_space_constraint(view_offsets[0, 0].T, pltpu.HBM), view_counts,
        jnp.asarray(np.concatenate([dft_tables(), order_tables()])),
    )


def solution(mesh):
    in_specs = (
        P(None, "row", "col"),
        P(),
        P("row", "col", None, None, None),
        P("row", "col", None, None),
        P("row", "col"),
    )
    out_specs = P(None, "row", "col")
    body = functools.partial(per_device, mesh.shape["row"], mesh.shape["col"])
    return jax.shard_map(body, mesh=mesh, in_specs=in_specs, out_specs=out_specs, check_vma=False)
```

```python
import functools

import jax
import jax.numpy as jnp
import ml_dtypes
import numpy as np
from jax import lax
from jax.experimental import pallas as pl
from jax.experimental.pallas import tpu as pltpu
from jax.sharding import PartitionSpec as P

MESH = pl.DeviceIdType.MESH
CORE = 256
MARGIN = 64
HALF = 128
smooth_eps = 0.1
step_size = 0.2
f32, bf16 = jnp.float32, jnp.bfloat16


def dft_tables():
    index = np.arange(HALF)
    forms = []
    for parity in (0, 1):
        turns = (index[:, None] * (2 * index[None, :] + parity)) % CORE
        entries = np.exp(-2j * np.pi * turns / CORE) / np.sqrt(CORE)
        forms.append(np.block([[entries.real, entries.imag], [-entries.imag, entries.real]]))
    forms = np.stack(forms).astype(np.float32)
    forms = np.stack([forms, np.swapaxes(forms, 1, 2)])
    high = forms.astype(ml_dtypes.bfloat16)
    low = (forms - high.astype(np.float32)).astype(ml_dtypes.bfloat16)
    return np.stack([high, low], axis=2).reshape(8, CORE, CORE)


def order_tables():
    move = np.zeros((CORE, CORE), np.float32)
    index = np.arange(HALF)
    move[2 * index, index] = 1.0
    move[2 * index + 1, HALF + index] = 1.0
    return np.stack([move, move.T]).astype(ml_dtypes.bfloat16)


def table(tab, form, parity, low):
    return tab[4 * form + 2 * parity + low]


def dot(left, right):
    return jnp.dot(left, right, preferred_element_type=f32)


def split(value):
    high = value.astype(bf16)
    return high, (value - high.astype(f32)).astype(bf16)


def times_table(value, tab, form, parity):
    high, low = split(value)
    t_high, t_low = table(tab, form, parity, 0), table(tab, form, parity, 1)
    return dot(high, t_high) + dot(low, t_high) + dot(high, t_low)


def table_times(value, tab, form, parity):
    high, low = split(value)
    t_high, t_low = table(tab, form, parity, 0), table(tab, form, parity, 1)
    return dot(t_high, high) + dot(t_high, low) + dot(t_low, high)


def lanes(*parts):
    return jnp.concatenate(parts, axis=1)


def rows(*parts):
    return jnp.concatenate(parts, axis=0)


def columns(tile):
    return slice(HALF * tile, HALF * tile + HALF)


def prepare_intensity(measured, tab, scaled, number):
    right, left = tab[8], tab[9]
    value = measured[number]
    first = value.astype(bf16)
    rest = value - first.astype(f32)
    second = rest.astype(bf16)
    third = (rest - second.astype(f32)).astype(bf16)
    moved = [dot(left, dot(part, right).astype(bf16)) for part in (first, second, third)]
    total = (moved[0] + moved[1] + moved[2]) + smooth_eps
    scaled[number, 0] = total[:HALF]
    scaled[number, 1] = total[HALF:]


def prepare_probe(probe, rolled, number, row_off, col_off):
    for part in range(2):
        turned = pltpu.roll(probe[part], lax.rem(row_off + CORE, CORE), 0)
        rolled[number, part] = pltpu.roll(turned, lax.rem(col_off + CORE, CORE), 1)


def one_view(number, row_off, col_off, valid, core, side, ends, corner, rolled, scaled, tab, sums):
    lane = lax.broadcasted_iota(jnp.int32, (1, HALF), 1)
    line = lax.broadcasted_iota(jnp.int32, (MARGIN, 1), 0)
    in_side = (lane < col_off, lane >= HALF + col_off)
    in_low, in_high = line < row_off, line >= MARGIN + row_off

    def patch(part, tile):
        middle = jnp.where(in_side[tile], side[part], core[part, :, columns(tile)])
        outer = jnp.where(in_side[tile], corner[part], ends[part, :, columns(tile)])
        low = jnp.where(in_low, outer[:64], middle[:64])
        high = jnp.where(in_high, outer[64:], middle[192:])
        return rows(low, middle[64:192], high)

    waves = []
    for tile in range(2):
        p_re, p_im = rolled[number, 0, :, columns(tile)], rolled[number, 1, :, columns(tile)]
        o_re, o_im = patch(0, tile), patch(1, tile)
        waves.append(lanes(p_re * o_re - p_im * o_im, p_re * o_im + p_im * o_re))
    yield
    even = times_table(waves[0] + waves[1], tab, 0, 0)
    odd = times_table(waves[0] - waves[1], tab, 0, 1)
    yield

    def stacked(even_cols, odd_cols):
        return rows(
            lanes(even_cols[:, :HALF], odd_cols[:, :HALF]),
            lanes(even_cols[:, HALF:], odd_cols[:, HALF:]),
        )

    halves = (
        stacked(even[:HALF] + even[HALF:], odd[:HALF] + odd[HALF:]),
        stacked(even[:HALF] - even[HALF:], odd[:HALF] - odd[HALF:]),
    )
    fars = [table_times(halves[parity], tab, 1, parity) for parity in range(2)]
    yield
    back = []
    for parity, far in enumerate(fars):
        far_re, far_im = far[:HALF], far[HALF:]
        wanted = scaled[number, parity]
        found = far_re * far_re + far_im * far_im + smooth_eps
        scaling = 1.0 - wanted * lax.rsqrt(wanted * found)
        corrected = rows(far_re * scaling, far_im * scaling)
        back.append(table_times(corrected, tab, 0, parity))
    yield
    upper, lower = back[0] + back[1], back[0] - back[1]
    re = rows(upper[:HALF], lower[:HALF])
    im = rows(upper[HALF:], lower[HALF:])
    even = times_table(lanes(re[:, :HALF], im[:, :HALF]), tab, 1, 0)
    odd = times_table(lanes(re[:, HALF:], im[:, HALF:]), tab, 1, 1)
    yield
    core_sum, side_sum, ends_sum, corner_sum = sums
    for tile, wave in ((0, even + odd), (1, even - odd)):
        b_re, b_im = wave[:, :HALF], wave[:, HALF:]
        p_re, p_im = rolled[number, 0, :, columns(tile)], rolled[number, 1, :, columns(tile)]
        for part, raw in ((0, p_re * b_re + p_im * b_im), (1, p_re * b_im - p_im * b_re)):
            grad = raw * valid
            outside = jnp.where(in_side[tile], grad, 0.0)
            for value, main, edge, where in (
                (grad - outside, core_sum, ends_sum, columns(tile)),
                (outside, side_sum, corner_sum, slice(0, HALF)),
            ):
                low = jnp.where(in_low, value[:64], 0.0)
                high = jnp.where(in_high, value[192:], 0.0)
                main[part, :64, where] = main[part, :64, where] + (value[:64] - low)
                main[part, 64:192, where] = main[part, 64:192, where] + value[64:192]
                main[part, 192:, where] = main[part, 192:, where] + (value[192:] - high)
                edge[part, :64, where] = edge[part, :64, where] + low
                edge[part, 64:, where] = edge[part, 64:, where] + high
    yield


BACK_CHUNKS = (64, 128, 0, 192)
BACK_VIA = (64, 0, 192)
RUN = 8
RELAY_AT = {("down", 0): 5, ("down", 1): 3, ("up", 0): 2, ("up", 1): 4}
CHUNKS = ((0, 64), (192, 64), (64, 128))


def step_kernel(
    n_row, n_col,
    object_hbm, probe_hbm, intensity_hbm, offsets_hbm, counts_hbm, tab_hbm,
    out_ref,
    core, probe, measured, tab, offsets, counts,
    pack, got, ends, corner_got, side, corner, rolled, scaled,
    core_sum, side_sum, ends_sum, corner_sum,
    back_pack, back_got, back_ends, back_corner,
    hold, back_hold,
    load_sem, send_sem, recv_sem,
):
    r, c = lax.axis_index("row"), lax.axis_index("col")
    has = {"left": c > 0, "right": c < n_col - 1, "up": r > 0, "down": r < n_row - 1}
    where = {"left": (r, c - 1), "right": (r, c + 1), "up": (r - 1, c), "down": (r + 1, c)}
    opposite = {"left": "right", "right": "left", "up": "down", "down": "up"}

    place = lax.rem(r, RUN)
    over = {"down": (place == RUN - 1) & has["down"], "up": (place == 0) & has["up"]}
    near = {way: has[way] & jnp.logical_not(over[way]) for way in over}
    has_run = {"down": r < n_row - RUN, "up": r >= RUN}
    relays = {key: (place == RELAY_AT[key]) & has_run[key[0]] for key in RELAY_AT}
    sign = {"down": 1, "up": -1}

    def row_at(offset):
        return (r + offset, c)

    def from_source(way, part):
        return -sign[way] * (2 * part + 2)

    def to_target(way, part):
        return sign[way] * (2 * part + 3)

    even = lax.rem(c, 2) == 0
    outward = {"left": even, "right": jnp.logical_not(even)}
    depth = jnp.where(even, c, n_col - 1 - c)
    beyond = (r, jnp.where(even, c - 2, c + 2))
    inner = (r, jnp.where(even, c + 2, c - 2))
    by_way = [(depth >= 2) & (depth <= n_col - 2 - 2 * level) for level in range(3)]
    passes = [depth <= n_col - 4 - 2 * level for level in range(3)]

    barrier = pltpu.get_barrier_semaphore()

    def greet(condition, device):
        @pl.when(condition)
        def _():
            pl.semaphore_signal(barrier, inc=1, device_id=device, device_id_type=MESH)

    greet(passes[0], inner)
    for way in where:
        greet(has[way], where[way])
    for way, part in RELAY_AT:
        greet(relays[way, part], row_at(-from_source(way, part)))
        greet(over[opposite[way]], row_at(-to_target(way, part)))

    loads = [
        pltpu.make_async_copy(source, target, load_sem.at[at])
        for at, (source, target) in enumerate((
            (object_hbm, core), (offsets_hbm, offsets), (counts_hbm, counts), (probe_hbm, probe),
            (intensity_hbm, measured), (tab_hbm, tab),
        ))
    ]
    for load in loads:
        load.start()

    def copy(at, device, source, target, arrival=None):
        return pltpu.make_async_remote_copy(
            src_ref=source, dst_ref=target, send_sem=send_sem.at[at],
            recv_sem=recv_sem.at[at if arrival is None else arrival], device_id=device, device_id_type=MESH,
        )

    sent = []

    def start(condition, made):
        sent.append((condition, made))

        @pl.when(condition)
        def _():
            made.start()

        return made

    def send(at, way, source, target):
        return start(has[way], copy(at, where[way], source, target))

    def send_chunk(at, way, source, target, held, via_at, level):
        straight = copy(at, where[way], source, target)
        if level is None:
            return start(has[way], straight)
        around = outward[way] & by_way[level]
        start(has[way] & jnp.logical_not(around), straight)
        start(around, copy(at, beyond, source, held, via_at + level))
        return straight

    def pass_chunk(numbers, targets, held, via_at, level):
        arriving = copy(via_at + 3 + level, inner, held, held, via_at + level)

        @pl.when(passes[level])
        def _():
            arriving.wait_recv()

        for way in ("left", "right"):
            made = copy(via_at + 3 + level, where[opposite[way]], held, targets[way], numbers[way])
            start(passes[level] & outward[way], made)

    def strip(ref, part, begin):
        return ref.at[part, pl.ds(begin, 64)]

    def send_ends(at, source, target, hold, begins):
        for way, (begin, end) in begins.items():
            for part in range(2):
                number = at + 2 * (way == "up") + part
                piece, spot = strip(source, part, begin), strip(target, part, end)
                start(near[way], copy(number, where[way], piece, spot))
                start(over[way], copy(number, row_at(from_source(way, part)), piece, hold, at + 4))

    def pass_ends(at, target, hold, begins):
        for way, part in RELAY_AT:
            number = at + 2 * (way == "up") + part
            spot = strip(target, part, begins[way][1])
            made = copy(at + 5, row_at(to_target(way, part)), hold, spot, number)
            arriving = copy(at + 5, row_at(to_target(way, part)), hold, hold, at + 4)

            @pl.when(relays[way, part])
            def _():
                arriving.wait_recv()

            start(relays[way, part], made)

    def receive_ends(at, way, source, target, begins):
        begin, end = begins[way]
        for part in range(2):
            number = at + 2 * (way == "up") + part
            receive(way, copy(number, where[way], strip(source, part, begin), strip(target, part, end)))

    def receive(way, made):
        @pl.when(has[opposite[way]])
        def _():
            made.wait_recv()

    zeros = jnp.zeros
    for way, spots in {
        "right": ((got, 0), (back_got, 1)),
        "left": ((got, 1), (back_got, 0)),
    }.items():
        @pl.when(jnp.logical_not(has[way]))
        def _():
            for ref, at in spots:
                ref[at] = zeros(ref.shape[1:], f32)
    for way, at in (("down", 0), ("up", 64)):
        @pl.when(jnp.logical_not(has[way]))
        def _():
            for ref in (ends, corner_got):
                ref[:, at : at + 64, :] = zeros((2, 64, ref.shape[2]), f32)
    for way, at in (("up", 0), ("down", 64)):
        @pl.when(jnp.logical_not(has[way]))
        def _():
            for ref in (back_ends, back_corner):
                ref[:, at : at + 64, :] = zeros((2, 64, ref.shape[2]), f32)
    for ref in (core_sum, side_sum, ends_sum, corner_sum):
        ref[...] = jnp.zeros_like(ref)

    first_half = lax.broadcasted_iota(jnp.int32, (1, HALF), 1) < MARGIN

    def turned(value):
        return pltpu.roll(value, MARGIN, 1)

    loads[0].wait()
    pack[0] = jnp.where(first_half, core[0, :, :HALF], turned(core[1, :, :HALF]))
    pack[1] = jnp.where(first_half, turned(core[0, :, HALF:]), core[1, :, HALF:])

    peers = sum(jnp.where(has[way], 1, 0) for way in where) + jnp.where(by_way[0], 1, 0)
    peers += sum(jnp.where(relays[key], 1, 0) + jnp.where(over[key[0]], 1, 0) for key in RELAY_AT)
    pl.semaphore_wait(barrier, peers)

    at = 0
    fore = {}
    for begin, size in CHUNKS:
        for slot, way in ((0, "left"), (1, "right")):
            part = pl.ds(begin, size)
            fore[begin, way] = send(at, way, pack.at[slot, part], got.at[slot, part])
            at += 1
    ends_at = at
    ends_begins = {"down": (192, 64), "up": (0, 0)}
    send_ends(ends_at, core, ends, hold, ends_begins)
    at += 6

    for load in loads[1:]:
        load.wait()
    for number in range(4):
        prepare_probe(probe, rolled, number, offsets[0, number] - MARGIN, offsets[1, number] - MARGIN)
    for number in range(4):
        prepare_intensity(measured, tab, scaled, number)

    for way in ("left", "right"):
        receive(way, fore[0, way])
    corner_up = send(at, "up", got.at[:, pl.ds(0, 64)], corner_got.at[:, pl.ds(0, 64)])
    pass_ends(ends_at, ends, hold, ends_begins)
    for way in ("left", "right"):
        receive(way, fore[192, way])
    corner_down = send(at + 1, "down", got.at[:, pl.ds(192, 64)], corner_got.at[:, pl.ds(64, 64)])
    at += 2
    for way in ("left", "right"):
        receive(way, fore[64, way])
    side[0] = jnp.where(first_half, got[0], turned(got[1]))
    side[1] = jnp.where(first_half, turned(got[0]), got[1])
    for way in ("down", "up"):
        receive_ends(ends_at, way, core, ends, ends_begins)
    receive("up", corner_up)
    receive("down", corner_down)
    corner[0] = jnp.where(first_half, corner_got[0], turned(corner_got[1]))
    corner[1] = jnp.where(first_half, turned(corner_got[0]), corner_got[1])

    def view(number):
        valid = jnp.where(number < counts[0, 0], 1.0, 0.0)
        return one_view(
            number, offsets[0, number] - MARGIN, offsets[1, number] - MARGIN, valid, core, side, ends, corner,
            rolled, scaled, tab, (core_sum, side_sum, ends_sum, corner_sum),
        )

    @pl.loop(0, 2)
    def _(pair):
        for _ in zip(view(2 * pair), view(2 * pair + 1)):
            pass

    grads = []
    for way, row in (("down", 0), ("up", 64)):
        part = pl.ds(row, 64)
        grads.append((way, row, send(at, way, corner_sum.at[:, part], back_corner.at[:, part])))
        at += 1
    back = {}

    def pack_sides(begin, size):
        part = slice(begin, begin + size)
        re, im = side_sum[0, part], side_sum[1, part]
        back_pack[0, part] = jnp.where(first_half, re, turned(im))
        back_pack[1, part] = jnp.where(first_half, turned(re), im)

    via_back = at
    at += 6
    numbers = {}

    def send_sides(begin):
        nonlocal at
        part = pl.ds(begin, 64)
        level = BACK_VIA.index(begin) if begin in BACK_VIA else None
        for slot, way in ((0, "right"), (1, "left")):
            numbers[begin, way] = at
            target = back_got.at[slot, part]
            back[begin, way] = send_chunk(at, way, back_pack.at[slot, part], target, back_hold.at[part], via_back, level)
            at += 1

    pack_sides(64, 128)
    send_sides(64)
    send_sides(128)
    edge = []
    for way, begin in (("down", 0), ("up", 64)):
        part = pl.ds(begin, 64)
        edge.append((way, begin, send(at, way, ends_sum.at[:, part], back_ends.at[:, part])))
        at += 1
    for way, row, made in grads:
        receive(way, made)
        begin = 0 if row == 0 else 192
        side_sum[:, begin : begin + 64] = side_sum[:, begin : begin + 64] + back_corner[:, row : row + 64]
        pack_sides(begin, 64)
        send_sides(begin)
    for level, begin in enumerate(BACK_VIA):
        part = pl.ds(begin, 64)
        targets = {"left": back_got.at[1, part], "right": back_got.at[0, part]}
        pass_chunk({way: numbers[begin, way] for way in targets}, targets, back_hold.at[part], via_back, level)
    for way, row, made in edge:
        receive(way, made)
        begin = 0 if row == 0 else 192
        core_sum[:, begin : begin + 64] = core_sum[:, begin : begin + 64] + back_ends[:, row : row + 64]
    out_ref[...] = core[...] - step_size * core_sum[...]
    for begin in BACK_CHUNKS:
        part = slice(begin, begin + 64)
        for way in ("right", "left"):
            receive(way, back[begin, way])
        from_left, from_right = back_got[0, part], back_got[1, part]
        for at_part, left_part, right_part in (
            (0, from_left, turned(from_right)),
            (1, turned(from_left), from_right),
        ):
            out_ref[at_part, part, :HALF] = out_ref[at_part, part, :HALF] - step_size * jnp.where(first_half, left_part, 0.0)
            out_ref[at_part, part, HALF:] = out_ref[at_part, part, HALF:] - step_size * jnp.where(first_half, 0.0, right_part)
    for condition, made in sent:
        @pl.when(condition)
        def _():
            made.wait_send()


def per_device(n_row, n_col, object_field, probe_field, intensity, view_offsets, view_counts):
    anywhere = pl.BlockSpec(memory_space=pl.ANY)
    vmem = pltpu.VMEM
    n_copies = 32
    return pl.pallas_call(
        functools.partial(step_kernel, n_row, n_col),
        out_shape=jax.ShapeDtypeStruct(object_field.shape, f32),
        in_specs=[anywhere] * 6,
        out_specs=pl.BlockSpec(memory_space=vmem),
        scratch_shapes=[
            vmem((2, 256, 256), f32), vmem((2, 256, 256), f32), vmem((4, 256, 256), f32),
            vmem((10, 256, 256), bf16),
            pltpu.SMEM((2, 4), jnp.int32), pltpu.SMEM((1, 1), jnp.int32),
            vmem((2, 256, 128), f32), vmem((2, 256, 128), f32), vmem((2, 128, 256), f32), vmem((2, 128, 128), f32),
            vmem((2, 256, 128), f32), vmem((2, 128, 128), f32),
            vmem((4, 2, 256, 256), f32), vmem((4, 2, 128, 256), f32),
            vmem((2, 256, 256), f32), vmem((2, 256, 128), f32), vmem((2, 128, 256), f32), vmem((2, 128, 128), f32),
            vmem((2, 256, 128), f32), vmem((2, 256, 128), f32), vmem((2, 128, 256), f32), vmem((2, 128, 128), f32),
            vmem((64, 256), f32), vmem((256, 128), f32),
            pltpu.SemaphoreType.DMA((6,)), pltpu.SemaphoreType.DMA((n_copies,)), pltpu.SemaphoreType.DMA((n_copies,)),
        ],
        compiler_params=pltpu.CompilerParams(
            collective_id=0, has_side_effects=True, vmem_limit_bytes=53 * 2**20
        ),
    )(
        object_field, probe_field, intensity[0, 0], pltpu.with_memory_space_constraint(view_offsets[0, 0].T, pltpu.HBM), view_counts,
        jnp.asarray(np.concatenate([dft_tables(), order_tables()])),
    )


def solution(mesh):
    in_specs = (
        P(None, "row", "col"),
        P(),
        P("row", "col", None, None, None),
        P("row", "col", None, None),
        P("row", "col"),
    )
    out_specs = P(None, "row", "col")
    body = functools.partial(per_device, mesh.shape["row"], mesh.shape["col"])
    return jax.shard_map(body, mesh=mesh, in_specs=in_specs, out_specs=out_specs, check_vma=False)
```

```python
import functools

import jax
import jax.numpy as jnp
import ml_dtypes
import numpy as np
from jax import lax
from jax.experimental import pallas as pl
from jax.experimental.pallas import tpu as pltpu
from jax.sharding import PartitionSpec as P

MESH = pl.DeviceIdType.MESH
CORE = 256
MARGIN = 64
HALF = 128
smooth_eps = 0.1
step_size = 0.2
f32, bf16 = jnp.float32, jnp.bfloat16


def dft_tables():
    index = np.arange(HALF)
    forms = []
    for parity in (0, 1):
        turns = (index[:, None] * (2 * index[None, :] + parity)) % CORE
        entries = np.exp(-2j * np.pi * turns / CORE) / np.sqrt(CORE)
        forms.append(np.block([[entries.real, entries.imag], [-entries.imag, entries.real]]))
    forms = np.stack(forms).astype(np.float32)
    forms = np.stack([forms, np.swapaxes(forms, 1, 2)])
    high = forms.astype(ml_dtypes.bfloat16)
    low = (forms - high.astype(np.float32)).astype(ml_dtypes.bfloat16)
    return np.stack([high, low], axis=2).reshape(8, CORE, CORE)


def order_tables():
    move = np.zeros((CORE, CORE), np.float32)
    index = np.arange(HALF)
    move[2 * index, index] = 1.0
    move[2 * index + 1, HALF + index] = 1.0
    return np.stack([move, move.T]).astype(ml_dtypes.bfloat16)


def table(tab, form, parity, low):
    return tab[4 * form + 2 * parity + low]


def dot(left, right):
    return jnp.dot(left, right, preferred_element_type=f32)


def split(value):
    high = value.astype(bf16)
    return high, (value - high.astype(f32)).astype(bf16)


def times_table(value, tab, form, parity):
    high, low = split(value)
    t_high, t_low = table(tab, form, parity, 0), table(tab, form, parity, 1)
    return dot(high, t_high) + dot(low, t_high) + dot(high, t_low)


def table_times(value, tab, form, parity):
    high, low = split(value)
    t_high, t_low = table(tab, form, parity, 0), table(tab, form, parity, 1)
    return dot(t_high, high) + dot(t_high, low) + dot(t_low, high)


def lanes(*parts):
    return jnp.concatenate(parts, axis=1)


def rows(*parts):
    return jnp.concatenate(parts, axis=0)


def columns(tile):
    return slice(HALF * tile, HALF * tile + HALF)


def prepare_intensity(measured, tab, scaled, number):
    right, left = tab[8], tab[9]
    value = measured[number]
    first = value.astype(bf16)
    rest = value - first.astype(f32)
    second = rest.astype(bf16)
    third = (rest - second.astype(f32)).astype(bf16)
    moved = [dot(left, dot(part, right).astype(bf16)) for part in (first, second, third)]
    total = (moved[0] + moved[1] + moved[2]) + smooth_eps
    scaled[number, 0] = total[:HALF]
    scaled[number, 1] = total[HALF:]


def prepare_probe(probe, rolled, number, row_off, col_off):
    for part in range(2):
        turned = pltpu.roll(probe[part], lax.rem(row_off + CORE, CORE), 0)
        rolled[number, part] = pltpu.roll(turned, lax.rem(col_off + CORE, CORE), 1)


def one_view(number, row_off, col_off, valid, core, side, ends, corner, rolled, scaled, tab, sums):
    lane = lax.broadcasted_iota(jnp.int32, (1, HALF), 1)
    line = lax.broadcasted_iota(jnp.int32, (MARGIN, 1), 0)
    in_side = (lane < col_off, lane >= HALF + col_off)
    in_low, in_high = line < row_off, line >= MARGIN + row_off

    def patch(part, tile):
        middle = jnp.where(in_side[tile], side[part], core[part, :, columns(tile)])
        outer = jnp.where(in_side[tile], corner[part], ends[part, :, columns(tile)])
        low = jnp.where(in_low, outer[:64], middle[:64])
        high = jnp.where(in_high, outer[64:], middle[192:])
        return rows(low, middle[64:192], high)

    waves = []
    for tile in range(2):
        p_re, p_im = rolled[number, 0, :, columns(tile)], rolled[number, 1, :, columns(tile)]
        o_re, o_im = patch(0, tile), patch(1, tile)
        waves.append(lanes(p_re * o_re - p_im * o_im, p_re * o_im + p_im * o_re))
    yield
    even = times_table(waves[0] + waves[1], tab, 0, 0)
    odd = times_table(waves[0] - waves[1], tab, 0, 1)
    yield

    def stacked(even_cols, odd_cols):
        return rows(
            lanes(even_cols[:, :HALF], odd_cols[:, :HALF]),
            lanes(even_cols[:, HALF:], odd_cols[:, HALF:]),
        )

    halves = (
        stacked(even[:HALF] + even[HALF:], odd[:HALF] + odd[HALF:]),
        stacked(even[:HALF] - even[HALF:], odd[:HALF] - odd[HALF:]),
    )
    fars = [table_times(halves[parity], tab, 1, parity) for parity in range(2)]
    yield
    back = []
    for parity, far in enumerate(fars):
        far_re, far_im = far[:HALF], far[HALF:]
        wanted = scaled[number, parity]
        found = far_re * far_re + far_im * far_im + smooth_eps
        scaling = 1.0 - wanted * lax.rsqrt(wanted * found)
        corrected = rows(far_re * scaling, far_im * scaling)
        back.append(table_times(corrected, tab, 0, parity))
    yield
    upper, lower = back[0] + back[1], back[0] - back[1]
    re = rows(upper[:HALF], lower[:HALF])
    im = rows(upper[HALF:], lower[HALF:])
    even = times_table(lanes(re[:, :HALF], im[:, :HALF]), tab, 1, 0)
    odd = times_table(lanes(re[:, HALF:], im[:, HALF:]), tab, 1, 1)
    yield
    core_sum, side_sum, ends_sum, corner_sum = sums
    for tile, wave in ((0, even + odd), (1, even - odd)):
        b_re, b_im = wave[:, :HALF], wave[:, HALF:]
        p_re, p_im = rolled[number, 0, :, columns(tile)], rolled[number, 1, :, columns(tile)]
        for part, raw in ((0, p_re * b_re + p_im * b_im), (1, p_re * b_im - p_im * b_re)):
            grad = raw * valid
            outside = jnp.where(in_side[tile], grad, 0.0)
            for value, main, edge, where in (
                (grad - outside, core_sum, ends_sum, columns(tile)),
                (outside, side_sum, corner_sum, slice(0, HALF)),
            ):
                low = jnp.where(in_low, value[:64], 0.0)
                high = jnp.where(in_high, value[192:], 0.0)
                main[part, :64, where] = main[part, :64, where] + (value[:64] - low)
                main[part, 64:192, where] = main[part, 64:192, where] + value[64:192]
                main[part, 192:, where] = main[part, 192:, where] + (value[192:] - high)
                edge[part, :64, where] = edge[part, :64, where] + low
                edge[part, 64:, where] = edge[part, 64:, where] + high
    yield


BACK_CHUNKS = (64, 128, 0, 192)
BACK_VIA = (64, 0, 192)
RUN = 8
RELAY_AT = {("down", 0): 5, ("down", 1): 3, ("up", 0): 2, ("up", 1): 4}
CHUNKS = ((0, 64), (192, 64), (64, 128))


def step_kernel(
    n_row, n_col,
    object_hbm, probe_hbm, intensity_hbm, offsets_hbm, counts_hbm, tab_hbm,
    out_ref,
    core, probe, measured, tab, offsets, counts,
    pack, got, ends, corner_got, side, corner, rolled, scaled,
    core_sum, side_sum, ends_sum, corner_sum,
    back_pack, back_got, back_ends, back_corner,
    hold, back_hold,
    load_sem, send_sem, recv_sem,
):
    r, c = lax.axis_index("row"), lax.axis_index("col")
    has = {"left": c > 0, "right": c < n_col - 1, "up": r > 0, "down": r < n_row - 1}
    where = {"left": (r, c - 1), "right": (r, c + 1), "up": (r - 1, c), "down": (r + 1, c)}
    opposite = {"left": "right", "right": "left", "up": "down", "down": "up"}

    place = lax.rem(r, RUN)
    over = {"down": (place == RUN - 1) & has["down"], "up": (place == 0) & has["up"]}
    near = {way: has[way] & jnp.logical_not(over[way]) for way in over}
    has_run = {"down": r < n_row - RUN, "up": r >= RUN}
    relays = {key: (place == RELAY_AT[key]) & has_run[key[0]] for key in RELAY_AT}
    sign = {"down": 1, "up": -1}

    def row_at(offset):
        return (r + offset, c)

    def from_source(way, part):
        return -sign[way] * (2 * part + 2)

    def to_target(way, part):
        return sign[way] * (2 * part + 3)

    even = lax.rem(c, 2) == 0
    outward = {"left": even, "right": jnp.logical_not(even)}
    depth = jnp.where(even, c, n_col - 1 - c)
    beyond = (r, jnp.where(even, c - 2, c + 2))
    inner = (r, jnp.where(even, c + 2, c - 2))
    by_way = [(depth >= 2) & (depth <= n_col - 2 - 2 * level) for level in range(3)]
    passes = [depth <= n_col - 4 - 2 * level for level in range(3)]

    barrier = pltpu.get_barrier_semaphore()

    def greet(condition, device):
        @pl.when(condition)
        def _():
            pl.semaphore_signal(barrier, inc=1, device_id=device, device_id_type=MESH)

    greet(passes[0], inner)
    for way in where:
        greet(has[way], where[way])
    for way, part in RELAY_AT:
        greet(relays[way, part], row_at(-from_source(way, part)))
        greet(over[opposite[way]], row_at(-to_target(way, part)))

    loads = [
        pltpu.make_async_copy(source, target, load_sem.at[at])
        for at, (source, target) in enumerate((
            (object_hbm, core), (offsets_hbm, offsets), (counts_hbm, counts), (probe_hbm, probe),
            (intensity_hbm, measured), (tab_hbm, tab),
        ))
    ]
    for load in loads:
        load.start()

    def copy(at, device, source, target, arrival=None):
        return pltpu.make_async_remote_copy(
            src_ref=source, dst_ref=target, send_sem=send_sem.at[at],
            recv_sem=recv_sem.at[at if arrival is None else arrival], device_id=device, device_id_type=MESH,
        )

    sent = []

    def start(condition, made):
        sent.append((condition, made))

        @pl.when(condition)
        def _():
            made.start()

        return made

    def send(at, way, source, target):
        return start(has[way], copy(at, where[way], source, target))

    def send_chunk(at, way, source, target, held, via_at, level):
        straight = copy(at, where[way], source, target)
        if level is None:
            return start(has[way], straight)
        around = outward[way] & by_way[level]
        start(has[way] & jnp.logical_not(around), straight)
        start(around, copy(at, beyond, source, held, via_at + level))
        return straight

    def pass_chunk(numbers, targets, held, via_at, level):
        arriving = copy(via_at + 3 + level, inner, held, held, via_at + level)

        @pl.when(passes[level])
        def _():
            arriving.wait_recv()

        for way in ("left", "right"):
            made = copy(via_at + 3 + level, where[opposite[way]], held, targets[way], numbers[way])
            start(passes[level] & outward[way], made)

    def strip(ref, part, begin):
        return ref.at[part, pl.ds(begin, 64)]

    def send_ends(at, source, target, hold, begins):
        for way, (begin, end) in begins.items():
            for part in range(2):
                number = at + 2 * (way == "up") + part
                piece, spot = strip(source, part, begin), strip(target, part, end)
                start(near[way], copy(number, where[way], piece, spot))
                start(over[way], copy(number, row_at(from_source(way, part)), piece, hold, at + 4))

    def pass_ends(at, target, hold, begins):
        for way, part in RELAY_AT:
            number = at + 2 * (way == "up") + part
            spot = strip(target, part, begins[way][1])
            made = copy(at + 5, row_at(to_target(way, part)), hold, spot, number)
            arriving = copy(at + 5, row_at(to_target(way, part)), hold, hold, at + 4)

            @pl.when(relays[way, part])
            def _():
                arriving.wait_recv()

            start(relays[way, part], made)

    def receive_ends(at, way, source, target, begins):
        begin, end = begins[way]
        for part in range(2):
            number = at + 2 * (way == "up") + part
            receive(way, copy(number, where[way], strip(source, part, begin), strip(target, part, end)))

    def receive(way, made):
        @pl.when(has[opposite[way]])
        def _():
            made.wait_recv()

    zeros = jnp.zeros
    for way, spots in {
        "right": ((got, 0), (back_got, 1)),
        "left": ((got, 1), (back_got, 0)),
    }.items():
        @pl.when(jnp.logical_not(has[way]))
        def _():
            for ref, at in spots:
                ref[at] = zeros(ref.shape[1:], f32)
    for way, at in (("down", 0), ("up", 64)):
        @pl.when(jnp.logical_not(has[way]))
        def _():
            for ref in (ends, corner_got):
                ref[:, at : at + 64, :] = zeros((2, 64, ref.shape[2]), f32)
    for way, at in (("up", 0), ("down", 64)):
        @pl.when(jnp.logical_not(has[way]))
        def _():
            for ref in (back_ends, back_corner):
                ref[:, at : at + 64, :] = zeros((2, 64, ref.shape[2]), f32)
    for ref in (core_sum, side_sum, ends_sum, corner_sum):
        ref[...] = jnp.zeros_like(ref)

    first_half = lax.broadcasted_iota(jnp.int32, (1, HALF), 1) < MARGIN

    def turned(value):
        return pltpu.roll(value, MARGIN, 1)

    loads[0].wait()
    pack[0] = jnp.where(first_half, core[0, :, :HALF], turned(core[1, :, :HALF]))
    pack[1] = jnp.where(first_half, turned(core[0, :, HALF:]), core[1, :, HALF:])

    peers = sum(jnp.where(has[way], 1, 0) for way in where) + jnp.where(by_way[0], 1, 0)
    peers += sum(jnp.where(relays[key], 1, 0) + jnp.where(over[key[0]], 1, 0) for key in RELAY_AT)
    pl.semaphore_wait(barrier, peers)

    at = 0
    fore = {}
    ends_at = at
    ends_begins = {"down": (192, 64), "up": (0, 0)}
    send_ends(ends_at, core, ends, hold, ends_begins)
    at += 6
    for begin, size in CHUNKS:
        for slot, way in ((0, "left"), (1, "right")):
            part = pl.ds(begin, size)
            fore[begin, way] = send(at, way, pack.at[slot, part], got.at[slot, part])
            at += 1

    for load in loads[1:]:
        load.wait()
    for number in range(4):
        prepare_probe(probe, rolled, number, offsets[0, number] - MARGIN, offsets[1, number] - MARGIN)
    for number in range(4):
        prepare_intensity(measured, tab, scaled, number)

    pass_ends(ends_at, ends, hold, ends_begins)
    for way in ("left", "right"):
        receive(way, fore[0, way])
    corner_up = send(at, "up", got.at[:, pl.ds(0, 64)], corner_got.at[:, pl.ds(0, 64)])
    for way in ("left", "right"):
        receive(way, fore[192, way])
    corner_down = send(at + 1, "down", got.at[:, pl.ds(192, 64)], corner_got.at[:, pl.ds(64, 64)])
    at += 2
    for way in ("left", "right"):
        receive(way, fore[64, way])
    side[0] = jnp.where(first_half, got[0], turned(got[1]))
    side[1] = jnp.where(first_half, turned(got[0]), got[1])
    for way in ("down", "up"):
        receive_ends(ends_at, way, core, ends, ends_begins)
    receive("up", corner_up)
    receive("down", corner_down)
    corner[0] = jnp.where(first_half, corner_got[0], turned(corner_got[1]))
    corner[1] = jnp.where(first_half, turned(corner_got[0]), corner_got[1])

    def view(number):
        valid = jnp.where(number < counts[0, 0], 1.0, 0.0)
        return one_view(
            number, offsets[0, number] - MARGIN, offsets[1, number] - MARGIN, valid, core, side, ends, corner,
            rolled, scaled, tab, (core_sum, side_sum, ends_sum, corner_sum),
        )

    @pl.loop(0, 2)
    def _(pair):
        for _ in zip(view(2 * pair), view(2 * pair + 1)):
            pass

    grads = []
    for way, row in (("down", 0), ("up", 64)):
        part = pl.ds(row, 64)
        grads.append((way, row, send(at, way, corner_sum.at[:, part], back_corner.at[:, part])))
        at += 1
    back = {}

    def pack_sides(begin, size):
        part = slice(begin, begin + size)
        re, im = side_sum[0, part], side_sum[1, part]
        back_pack[0, part] = jnp.where(first_half, re, turned(im))
        back_pack[1, part] = jnp.where(first_half, turned(re), im)

    via_back = at
    at += 6
    numbers = {}

    def send_sides(begin):
        nonlocal at
        part = pl.ds(begin, 64)
        level = BACK_VIA.index(begin) if begin in BACK_VIA else None
        for slot, way in ((0, "right"), (1, "left")):
            numbers[begin, way] = at
            target = back_got.at[slot, part]
            back[begin, way] = send_chunk(at, way, back_pack.at[slot, part], target, back_hold.at[part], via_back, level)
            at += 1

    pack_sides(64, 128)
    send_sides(64)
    send_sides(128)
    edge = []
    for way, begin in (("down", 0), ("up", 64)):
        part = pl.ds(begin, 64)
        edge.append((way, begin, send(at, way, ends_sum.at[:, part], back_ends.at[:, part])))
        at += 1
    for way, row, made in grads:
        receive(way, made)
        begin = 0 if row == 0 else 192
        side_sum[:, begin : begin + 64] = side_sum[:, begin : begin + 64] + back_corner[:, row : row + 64]
        pack_sides(begin, 64)
        send_sides(begin)
    for level, begin in enumerate(BACK_VIA):
        part = pl.ds(begin, 64)
        targets = {"left": back_got.at[1, part], "right": back_got.at[0, part]}
        pass_chunk({way: numbers[begin, way] for way in targets}, targets, back_hold.at[part], via_back, level)
    for way, row, made in edge:
        receive(way, made)
        begin = 0 if row == 0 else 192
        core_sum[:, begin : begin + 64] = core_sum[:, begin : begin + 64] + back_ends[:, row : row + 64]
    out_ref[...] = core[...] - step_size * core_sum[...]
    for begin in BACK_CHUNKS:
        part = slice(begin, begin + 64)
        for way in ("right", "left"):
            receive(way, back[begin, way])
        from_left, from_right = back_got[0, part], back_got[1, part]
        for at_part, left_part, right_part in (
            (0, from_left, turned(from_right)),
            (1, turned(from_left), from_right),
        ):
            out_ref[at_part, part, :HALF] = out_ref[at_part, part, :HALF] - step_size * jnp.where(first_half, left_part, 0.0)
            out_ref[at_part, part, HALF:] = out_ref[at_part, part, HALF:] - step_size * jnp.where(first_half, 0.0, right_part)
    for condition, made in sent:
        @pl.when(condition)
        def _():
            made.wait_send()


def per_device(n_row, n_col, object_field, probe_field, intensity, view_offsets, view_counts):
    anywhere = pl.BlockSpec(memory_space=pl.ANY)
    vmem = pltpu.VMEM
    n_copies = 32
    return pl.pallas_call(
        functools.partial(step_kernel, n_row, n_col),
        out_shape=jax.ShapeDtypeStruct(object_field.shape, f32),
        in_specs=[anywhere] * 6,
        out_specs=pl.BlockSpec(memory_space=vmem),
        scratch_shapes=[
            vmem((2, 256, 256), f32), vmem((2, 256, 256), f32), vmem((4, 256, 256), f32),
            vmem((10, 256, 256), bf16),
            pltpu.SMEM((2, 4), jnp.int32), pltpu.SMEM((1, 1), jnp.int32),
            vmem((2, 256, 128), f32), vmem((2, 256, 128), f32), vmem((2, 128, 256), f32), vmem((2, 128, 128), f32),
            vmem((2, 256, 128), f32), vmem((2, 128, 128), f32),
            vmem((4, 2, 256, 256), f32), vmem((4, 2, 128, 256), f32),
            vmem((2, 256, 256), f32), vmem((2, 256, 128), f32), vmem((2, 128, 256), f32), vmem((2, 128, 128), f32),
            vmem((2, 256, 128), f32), vmem((2, 256, 128), f32), vmem((2, 128, 256), f32), vmem((2, 128, 128), f32),
            vmem((64, 256), f32), vmem((256, 128), f32),
            pltpu.SemaphoreType.DMA((6,)), pltpu.SemaphoreType.DMA((n_copies,)), pltpu.SemaphoreType.DMA((n_copies,)),
        ],
        compiler_params=pltpu.CompilerParams(
            collective_id=0, has_side_effects=True, vmem_limit_bytes=53 * 2**20
        ),
    )(
        object_field, probe_field, intensity[0, 0], pltpu.with_memory_space_constraint(view_offsets[0, 0].T, pltpu.HBM), view_counts,
        jnp.asarray(np.concatenate([dft_tables(), order_tables()])),
    )


def solution(mesh):
    in_specs = (
        P(None, "row", "col"),
        P(),
        P("row", "col", None, None, None),
        P("row", "col", None, None),
        P("row", "col"),
    )
    out_specs = P(None, "row", "col")
    body = functools.partial(per_device, mesh.shape["row"], mesh.shape["col"])
    return jax.shard_map(body, mesh=mesh, in_specs=in_specs, out_specs=out_specs, check_vma=False)
```
